256 devices in a mesh: phase: 8 (over y, x_hi), slab: 32 (over x_lo, z, core).
Axes of the slice: x: 4 (x_hi: 2, x_lo: 2; x = x_hi * 2 + x_lo), y: 4, z: 8, core: 2. Of those that a mesh axis runs over, the one named last changes fastest.
Arguments:
- images: float32 [16, 1024, 64, 128], P('phase', 'slab'), may hold values from -8 to 8, as said below
Outputs:
- forces: float32 [3, 16, 1024, 64, 128], P(None, 'phase', 'slab')
The draws below stay inside these ranges and needn't reach their ends.
Inputs may be any that keep to these rules, and one draw needn't show every extreme that they name: `images`: Breathing-phase volumes of one body.
All inputs are finite; a program needn't handle non-finite values.
Results may differ from the reference program's by a relative error of at most 0.0001.
Values sent between devices are 32-bit elements; how exact they have to be, the bound alone decides.
A program may use at most 128 MiB of HBM per device.

```python
import jax
import jax.numpy as jnp
from jax import lax

CY = 64
CX = 128
PHASES = 16
NZ = 1024


def draw_images(key, part):
    shape = (PHASES, NZ, CY, CX)
    anatomy_key = jax.random.fold_in(key, 11)
    noise_key = jax.random.fold_in(key, 23)
    scale_key = jax.random.fold_in(key, 37)
    anatomy = jax.random.normal(anatomy_key, (NZ, CY, CX), jnp.float32)
    noise = 0.6 * jax.random.normal(noise_key, shape, jnp.float32)
    scales = jax.random.uniform(scale_key, (PHASES,), jnp.float32, 0.8, 1.2)
    images = scales[:, None, None, None] * anatomy[None] + noise
    return jnp.clip(images, -8.0, 8.0)


def setup_inputs(seed: int = 0) -> dict:
    keys = jax.random.split(jax.random.key(seed), 2)
    return {
        "images": draw_images(jax.random.fold_in(keys[1], 71), 0),
    }


EPSILON = 1e-5


def window_mean(field):
    summed = field
    for direction in range(3):
        widths = [(4, 4) if dimension == direction else (0, 0) for dimension in range(3)]
        padded = jnp.pad(summed, widths)
        length = summed.shape[direction]
        summed = sum(lax.slice_in_dim(padded, offset, offset + length, axis=direction) for offset in range(9))
    return summed / 729.0


def pair_terms(left_field, right_field):
    mean_left = window_mean(left_field)
    mean_right = window_mean(right_field)
    spread_left = window_mean(left_field * left_field) - mean_left * mean_left
    spread_right = window_mean(right_field * right_field) - mean_right * mean_right
    covariance = window_mean(left_field * right_field) - mean_left * mean_right
    offset_left = left_field - mean_left
    offset_right = right_field - mean_right
    weight = 2.0 * covariance / (spread_left * spread_right + EPSILON)
    toward_left = weight * (offset_right - covariance / (spread_left + EPSILON) * offset_left)
    toward_right = weight * (offset_left - covariance / (spread_right + EPSILON) * offset_right)
    return toward_left, toward_right


def gradient(field):
    padded = jnp.pad(field, 1)
    along_z = (padded[2:, 1:-1, 1:-1] - padded[:-2, 1:-1, 1:-1]) * 0.5
    along_y = (padded[1:-1, 2:, 1:-1] - padded[1:-1, :-2, 1:-1]) * 0.5
    along_x = (padded[1:-1, 1:-1, 2:] - padded[1:-1, 1:-1, :-2]) * 0.5
    return jnp.stack([along_z, along_y, along_x])


def reference(images):
    coefs = jnp.zeros_like(images)
    for distance in (1, 2):
        partner = jnp.roll(images, -distance, axis=0)
        toward_own, toward_partner = lax.map(lambda couple: pair_terms(couple[0], couple[1]), (images, partner))
        coefs = coefs + toward_own + jnp.roll(toward_partner, distance, axis=0)
    forces = lax.map(lambda couple: gradient(couple[0]) * couple[1][None], (images, coefs))
    return jnp.transpose(forces, (1, 0, 2, 3, 4))
```

```python
import functools

import jax
import jax.numpy as jnp
from jax import lax
from jax.experimental import pallas as pl
from jax.experimental.pallas import tpu as pltpu
from jax.sharding import PartitionSpec as P

EPSILON = 1e-05
MESH = pl.DeviceIdType.MESH
PAIRS = ((2, 3), (2, 4), (2, 1), (2, 0), (3, 4), (3, 5), (3, 1))
FIELDS = 12 + len(PAIRS)
CY, CX = 64, 128
DEPTH = 32
BLOCK = 4


def plane_windows(at, buf, padded, partial, operand, band, windows):
    values = [buf[j, at] for j in range(6)]
    for f in range(FIELDS):
        if f < 6:
            field = values[f]
        elif f < 12:
            field = values[f - 6] * values[f - 6]
        else:
            a, b = PAIRS[f - 12]
            field = values[a] * values[b]
        padded[f, 8:72, :] = field
    for f in range(FIELDS):
        partial[f] = padded[f, 3:75, :] + padded[f, 4:76, :] + padded[f, 5:77, :]
    for f in range(FIELDS):
        summed = partial[f, 1:65, :] + partial[f, 4:68, :] + partial[f, 7:71, :]
        high = summed.astype(jnp.bfloat16)
        rest = summed - high.astype(jnp.float32)
        middle = rest.astype(jnp.bfloat16)
        low = (rest - middle.astype(jnp.float32)).astype(jnp.bfloat16)
        rows = slice(f * CY, (f + 1) * CY)
        operand[rows, 0:128] = high
        operand[rows, 128:256] = middle
        operand[rows, 256:384] = low
    windows[at] = jnp.dot(operand[...], band[...], preferred_element_type=jnp.float32)


def block_coefs(c, buf, windows, coef_ref):
    first = c * BLOCK

    @pl.loop(0, CY // 8)
    def _(r):
        sums = []
        for f in range(FIELDS):
            rows = pl.ds(pl.multiple_of(f * CY + r * 8, 8), 8)
            p = [windows[first + i, rows, :] for i in range(12)]
            common = (p[3] + p[4]) + (p[5] + p[6]) + (p[7] + p[8])
            left = p[1] + p[2]
            right = p[9] + p[10]
            sums.append(
                [common + (p[0] + left), common + (left + p[9]), common + (p[2] + right), common + (right + p[11])]
            )
        tile = pl.ds(pl.multiple_of(r * 8, 8), 8)
        for i in range(BLOCK):
            total = [s[i] * (1.0 / 729.0) for s in sums]
            mean = total[:6]
            spread = [total[6 + j] - mean[j] * mean[j] for j in range(6)]
            offset = [buf[j, first + 4 + i, tile, :] - mean[j] for j in range(6)]
            along = {2: 0.0, 3: 0.0}
            across = {2: 0.0, 3: 0.0}
            for k, (a, b) in enumerate(PAIRS):
                covariance = total[12 + k] - mean[a] * mean[b]
                weight = 2.0 * covariance / (spread[a] * spread[b] + EPSILON)
                scaled = weight * covariance
                along[a] += weight * offset[b]
                across[a] += scaled
                if b == 3:
                    along[b] += weight * offset[a]
                    across[b] += scaled
            for own in (2, 3):
                coef_ref[own - 2, first + i, tile, :] = (
                    along[own] - across[own] / (spread[own] + EPSILON) * offset[own]
                )


def coef_kernel(
    images, coef_ref, rim_ref, buf, padded, partial, operand, band, windows,
    x_send, x_recv, y_send, y_recv, rim_send, rim_recv, local_sem,
):
    phase, slab = lax.axis_index("phase"), lax.axis_index("slab")
    slabs = lax.axis_size("slab")
    y, side = phase // 2, phase % 2
    partner = (y * 2 + 1 - side, slab)
    y_to = ((y + 1 + 2 * side) % 4 * 2 + side, slab)
    y_from = ((y + 3 + 2 * side) % 4 * 2 + side, slab)
    below = (phase, (slab + slabs - 1) % slabs)
    above = (phase, (slab + 1) % slabs)

    barrier = pltpu.get_barrier_semaphore()
    for peer in (partner, y_to, y_from, below, above):
        pl.semaphore_signal(barrier, inc=1, device_id=peer, device_id_type=MESH)
    pl.semaphore_wait(barrier, 5)

    from_x, from_y = 4 - 4 * side, 4 * side

    def plane_of(k):
        return (k + DEPTH - 4) % DEPTH

    def x_copy(k, slot):
        z = plane_of(k)
        return pltpu.make_async_remote_copy(
            images.at[:, pl.ds(z, 1)], buf.at[pl.ds(slot, 2), pl.ds(4 + z, 1)],
            x_send.at[k], x_recv.at[k], device_id=partner, device_id_type=MESH,
        )

    def y_copy(k):
        z = plane_of(k)
        return pltpu.make_async_remote_copy(
            buf.at[pl.ds(from_x, 2), pl.ds(4 + z, 1)], buf.at[pl.ds(from_y, 2), pl.ds(4 + z, 1)],
            y_send.at[k], y_recv.at[k], device_id=y_to, device_id_type=MESH,
        )

    def rim_copy(which, up):
        slot = (2, from_x, from_y)[which]
        source = pl.ds(DEPTH, 4) if up else pl.ds(4, 4)
        target = pl.ds(0, 4) if up else pl.ds(DEPTH + 4, 4)
        return pltpu.make_async_remote_copy(
            buf.at[pl.ds(slot, 2), source], buf.at[pl.ds(slot, 2), target],
            rim_send.at[which, up], rim_recv.at[which, up],
            device_id=above if up else below, device_id_type=MESH,
        )

    def each_rim(whiches, ups, act, arriving):
        for up in ups:
            edge = (0 if arriving else slabs - 1) if up else (slabs - 1 if arriving else 0)

            @pl.when(slab != edge)
            def _():
                for which in whiches:
                    act(rim_copy(which, up))

    @pl.loop(0, DEPTH)
    def _(k):
        x_copy(k, from_y).start()

    own = pltpu.make_async_copy(images, buf.at[pl.ds(2, 2), pl.ds(4, DEPTH)], local_sem)
    own.start()

    @pl.when(slab == 0)
    def _():
        buf[:, 0:4] = jnp.zeros((6, 4, CY, CX), jnp.float32)

    @pl.when(slab == slabs - 1)
    def _():
        buf[:, DEPTH + 4 : DEPTH + 8] = jnp.zeros((6, 4, CY, CX), jnp.float32)

    padded[:, 0:8, :] = jnp.zeros((FIELDS, 8, CX), jnp.float32)
    padded[:, 72:80, :] = jnp.zeros((FIELDS, 8, CX), jnp.float32)
    row = lax.broadcasted_iota(jnp.int32, (128, 128), 0)
    column = lax.broadcasted_iota(jnp.int32, (128, 128), 1)
    near = jnp.where(jnp.abs(row - column) <= 4, 1.0, 0.0).astype(jnp.bfloat16)
    for i in range(3):
        band[i * 128 : (i + 1) * 128, :] = near
    own.wait()
    each_rim((0,), (0, 1), lambda copy: copy.start(), False)

    def serve(k):
        x_copy(k, from_x).wait_recv()
        y_copy(k).start()

    serve(0)

    @pl.loop(0, DEPTH)
    def _(u):
        @pl.when(u < DEPTH - 1)
        def _():
            serve(u + 1)

        y_copy(u).wait_recv()

        @pl.when(u == 3)
        def _():
            each_rim((1, 2), (1,), lambda copy: copy.start(), False)

        @pl.when(u == 7)
        def _():
            each_rim((1, 2), (0,), lambda copy: copy.start(), False)

        @pl.when(u == 16)
        def _():
            each_rim((0, 1, 2), (0, 1), lambda copy: copy.wait_recv(), True)

        eighth = u // 8
        twice = eighth // 2 * (1 - eighth % 2)

        @pl.loop(0, 1 + twice)
        def _(w):
            r = (u - 16) * w
            at = (1 - w) * (plane_of(u) + 4) + w * (r + DEPTH * (r // 4))
            plane_windows(at, buf, padded, partial, operand, band, windows)

        @pl.when((u >= 24) & (u < 29))
        def _():
            block_coefs(u - 24, buf, windows, coef_ref)

    @pl.loop(5, DEPTH // BLOCK)
    def _(c):
        block_coefs(c, buf, windows, coef_ref)

    rim_ref[:, 0] = buf[2:4, 3]
    rim_ref[:, 1] = buf[2:4, DEPTH + 4]

    @pl.loop(0, DEPTH)
    def _(k):
        x_copy(k, from_y).wait_send()
        y_copy(k).wait_send()

    each_rim((0, 1, 2), (0, 1), lambda copy: copy.wait_send(), False)


def force_kernel(depth, coef_ref, image_ref, below_ref, above_ref, rim_ref, out_ref):
    j, last = pl.program_id(1), pl.num_programs(1) - 1
    below = jnp.where(j == 0, rim_ref[0, 0], below_ref[0, 0])
    above = jnp.where(j == last, rim_ref[0, 1], above_ref[0, 0])
    row = lax.broadcasted_iota(jnp.int32, (CY, CX), 0)
    column = lax.broadcasted_iota(jnp.int32, (CY, CX), 1)
    for i in range(depth):
        half = coef_ref[0, i] * 0.5
        here = image_ref[0, i]
        up = image_ref[0, i + 1] if i + 1 < depth else above
        down = image_ref[0, i - 1] if i else below
        out_ref[0, 0, i] = half * (up - down)
        up = jnp.where(row < CY - 1, pltpu.roll(here, CY - 1, 0), 0.0)
        down = jnp.where(row > 0, pltpu.roll(here, 1, 0), 0.0)
        out_ref[1, 0, i] = half * (up - down)
        up = jnp.where(column < CX - 1, pltpu.roll(here, CX - 1, 1), 0.0)
        down = jnp.where(column > 0, pltpu.roll(here, 1, 1), 0.0)
        out_ref[2, 0, i] = half * (up - down)


def local(images):
    f32, vmem = jnp.float32, pl.BlockSpec(memory_space=pltpu.VMEM)
    dma = pltpu.SemaphoreType.DMA
    coefs, rims = pl.pallas_call(
        coef_kernel,
        out_shape=(
            jax.ShapeDtypeStruct((2, DEPTH, CY, CX), f32),
            jax.ShapeDtypeStruct((2, 2, CY, CX), f32),
        ),
        in_specs=[pl.BlockSpec(memory_space=pl.ANY)],
        out_specs=(vmem, vmem),
        scratch_shapes=[
            pltpu.VMEM((6, DEPTH + 8, CY, CX), f32),
            pltpu.VMEM((FIELDS, 80, CX), f32),
            pltpu.VMEM((FIELDS, 72, CX), f32),
            pltpu.VMEM((FIELDS * CY, 384), jnp.bfloat16),
            pltpu.VMEM((384, CX), jnp.bfloat16),
            pltpu.VMEM((DEPTH + 8, FIELDS * CY, CX), f32),
            dma((DEPTH,)), dma((DEPTH,)), dma((DEPTH,)), dma((DEPTH,)),
            dma((3, 2)), dma((3, 2)), dma,
        ],
        compiler_params=pltpu.CompilerParams(
            collective_id=0, has_side_effects=True, vmem_limit_bytes=56 * 2**20
        ),
        name="coefs",
    )(images)
    depth = 8
    block = (1, depth, CY, CX)
    plane = (1, 1, CY, CX)
    return pl.pallas_call(
        functools.partial(force_kernel, depth),
        out_shape=jax.ShapeDtypeStruct((3, 2, DEPTH, CY, CX), f32),
        grid=(2, DEPTH // depth),
        in_specs=[
            pl.BlockSpec(block, lambda p, j: (p, j, 0, 0)),
            pl.BlockSpec(block, lambda p, j: (p, j, 0, 0)),
            pl.BlockSpec(plane, lambda p, j: (p, jnp.maximum(j * depth - 1, 0), 0, 0)),
            pl.BlockSpec(plane, lambda p, j: (p, jnp.minimum(j * depth + depth, DEPTH - 1), 0, 0)),
            pl.BlockSpec((1, 2, CY, CX), lambda p, j: (p, 0, 0, 0)),
        ],
        out_specs=pl.BlockSpec((3, 1, depth, CY, CX), lambda p, j: (0, p, j, 0, 0)),
        name="forces",
    )(coefs, images, images, images, rims)


def solution(mesh):
    in_specs = (P("phase", "slab", None, None),)
    out_specs = P(None, "phase", "slab", None, None)
    return jax.shard_map(local, mesh=mesh, in_specs=in_specs, out_specs=out_specs, check_vma=False)
```

```python
import jax
import jax.numpy as jnp
from jax import lax
from jax.experimental import pallas as pl
from jax.experimental.pallas import tpu as pltpu
from jax.sharding import PartitionSpec as P

EPSILON = 1e-05
MESH = pl.DeviceIdType.MESH
SOON = (0, 1, 2, 3, (0, 0), (1, 1), (2, 2), (3, 3), (0, 1), (0, 2), (1, 2), (1, 3))
LATE = (4, 5, (4, 4), (5, 5), (0, 5), (0, 4), (1, 5))
ORDER = SOON + LATE
PAIRS = tuple(f for f in ORDER if f not in range(6) and f[0] != f[1])
FIELDS = len(ORDER)
CY, CX = 64, 128
DEPTH = 32
SENT = {(1, 1): 0, (2, 1): 3, (1, 0): 4, (2, 0): 7}
RELAY = 6
BLOCKS = ((0, 7, 20), (7, 8, 24), (15, 4, 27), (19, 4, 30))
LAST = 23
STORE = 4
LAG = 4


def plane_windows(fields, at, place, buf, padded, partial, operand, band, windows):
    base, count = ORDER.index(fields[0]), len(fields)
    images = {j: buf[place[j], at] for j in range(6) if any(j == f or f not in range(6) and j in f for f in fields)}
    for f, field in enumerate(fields, base):
        padded[f, 8:72, :] = images[field] if field in range(6) else images[field[0]] * images[field[1]]
    for f in range(base, base + count):
        partial[f] = padded[f, 3:75, :] + padded[f, 4:76, :] + padded[f, 5:77, :]
    for f in range(base, base + count):
        summed = partial[f, 1:65, :] + partial[f, 4:68, :] + partial[f, 7:71, :]
        high = summed.astype(jnp.bfloat16)
        rest = summed - high.astype(jnp.float32)
        middle = rest.astype(jnp.bfloat16)
        low = (rest - middle.astype(jnp.float32)).astype(jnp.bfloat16)
        rows = slice(f * CY, (f + 1) * CY)
        operand[rows, 0:128] = high
        operand[rows, 128:256] = middle
        operand[rows, 256:384] = low
    rows = slice(base * CY, (base + count) * CY)
    windows[at, rows] = jnp.dot(operand[rows, :], band[...], preferred_element_type=jnp.float32)


def block_coefs(first, size, place, buf, windows, coef_ref):
    @pl.loop(0, CY // 8)
    def _(r):
        sums = []
        for f in range(FIELDS):
            p = windows[pl.ds(first, size + 8), pl.ds(pl.multiple_of(f * CY + r * 8, 8), 8), :]
            common = p[size - 1]
            for i in range(size, 9):
                common = common + p[i]
            left, right = {}, {}
            for i in reversed(range(size - 1)):
                left[i] = p[i] + left[i + 1] if i + 1 in left else p[i]
            for i in range(1, size):
                right[i] = right[i - 1] + p[8 + i] if i - 1 in right else p[8 + i]
            sums.append([])
            for i in range(size):
                ends = [part[i] for part in (left, right) if i in part]
                sums[f].append(common + (ends[0] + ends[1] if len(ends) == 2 else ends[0]))
        tile = pl.ds(pl.multiple_of(r * 8, 8), 8)
        for i in range(size):
            total = {field: s[i] * (1.0 / 729.0) for field, s in zip(ORDER, sums)}
            spread = [total[j, j] - total[j] * total[j] for j in range(6)]
            offset = [buf[place[j], first + 4 + i, tile, :] - total[j] for j in range(6)]
            along, across = [0.0, 0.0], [0.0, 0.0]
            for a, b in PAIRS:
                covariance = total[a, b] - total[a] * total[b]
                weight = 2.0 * covariance / (spread[a] * spread[b] + EPSILON)
                scaled = weight * covariance
                for own, other in ((a, b), (b, a)):
                    if own < 2:
                        along[own] += weight * offset[other]
                        across[own] += scaled
            for own in (0, 1):
                coef_ref[place[own] - 2, first + i, tile, :] = (
                    along[own] - across[own] / (spread[own] + EPSILON) * offset[own]
                )


def coef_kernel(
    images, coef_ref, gradient_ref, buf, padded, partial, operand, band, windows,
    x_send, x_recv, y_send, y_recv, rim_send, rim_recv, relay_send, relay_recv, local_sem, relay,
):
    phase, slab = lax.axis_index("phase"), lax.axis_index("slab")
    slabs = lax.axis_size("slab")
    y, side = phase // 2, phase % 2
    partner = (y * 2 + 1 - side, slab)
    y_to = ((y + 1 + 2 * side) % 4 * 2 + side, slab)
    y_from = ((y + 3 + 2 * side) % 4 * 2 + side, slab)
    below = (phase, (slab + slabs - 1) % slabs)
    above = (phase, (slab + 1) % slabs)

    barrier = pltpu.get_barrier_semaphore()
    for peer in (partner, y_to, y_from, below, above):
        pl.semaphore_signal(barrier, inc=1, device_id=peer, device_id_type=MESH)

    middle = slabs // 2
    relays = {(1, 1): middle + 2, (2, 1): slabs - 4, (1, 0): middle - 3, (2, 0): 3}
    ends = (slab == middle - 1) | (slab == middle)
    passes = (slab == middle + 2) | (slab == slabs - 4) | (slab == middle - 3) | (slab == 3)

    @pl.when(ends)
    def _():
        for peer in relays.values():
            pl.semaphore_signal(barrier, inc=1, device_id=(phase, peer), device_id_type=MESH)
        pl.semaphore_wait(barrier, 9)

    @pl.when(passes)
    def _():
        for peer in (middle - 1, middle):
            pl.semaphore_signal(barrier, inc=1, device_id=(phase, peer), device_id_type=MESH)
        pl.semaphore_wait(barrier, 7)

    @pl.when(jnp.logical_not(ends | passes))
    def _():
        pl.semaphore_wait(barrier, 5)

    from_x, from_y = 4 - 4 * side, 4 * side
    place = (2 + side, 3 - side, from_x + side, from_x + 1 - side, from_y + side, from_y + 1 - side)

    def plane_of(k):
        return (k + DEPTH - 4) % DEPTH

    def x_copy(k, slot):
        z = plane_of(k)
        return pltpu.make_async_remote_copy(
            images.at[:, pl.ds(z, 1)], buf.at[pl.ds(slot, 2), pl.ds(4 + z, 1)],
            x_send.at[k], x_recv.at[k], device_id=partner, device_id_type=MESH,
        )

    def y_copy(k):
        z = plane_of(k)
        return pltpu.make_async_remote_copy(
            buf.at[pl.ds(from_x, 2), pl.ds(4 + z, 1)], buf.at[pl.ds(from_y, 2), pl.ds(4 + z, 1)],
            y_send.at[k], y_recv.at[k], device_id=y_to, device_id_type=MESH,
        )

    def rim_copy(which, up):
        slot = (2, from_x, from_y)[which]
        source = pl.ds(DEPTH, 4) if up else pl.ds(4, 4)
        target = pl.ds(0, 4) if up else pl.ds(DEPTH + 4, 4)
        return pltpu.make_async_remote_copy(
            buf.at[pl.ds(slot, 2), source], buf.at[pl.ds(slot, 2), target],
            rim_send.at[which, up], rim_recv.at[which, up],
            device_id=above if up else below, device_id_type=MESH,
        )

    def to_relay(which, up):
        slot = (2, from_x, from_y)[which]
        return pltpu.make_async_remote_copy(
            buf.at[pl.ds(slot, 2), pl.ds(DEPTH, 4) if up else pl.ds(4, 4)], relay,
            relay_send.at[which], relay_recv, device_id=(phase, relays[which, up]), device_id_type=MESH,
        )

    def from_relay(which, up):
        slot = (2, from_x, from_y)[which]
        return pltpu.make_async_remote_copy(
            relay, buf.at[pl.ds(slot, 2), pl.ds(0, 4) if up else pl.ds(DEPTH + 4, 4)],
            relay_send.at[0], rim_recv.at[which, up],
            device_id=(phase, middle if up else middle - 1), device_id_type=MESH,
        )

    def send_rims(whiches, up, act):
        edge, end = (slabs - 1, middle - 1) if up else (0, middle)

        @pl.when((slab != edge) & (slab != end))
        def _():
            for which in whiches:
                act(rim_copy(which, up))

        @pl.when(slab == end)
        def _():
            for which in whiches:
                act(to_relay(which, up) if which else rim_copy(which, up))

    def await_rims(whiches, up):
        @pl.when(slab != (0 if up else slabs - 1))
        def _():
            for which in whiches:
                rim_copy(which, up).wait_recv()

    @pl.loop(0, DEPTH)
    def _(k):
        x_copy(k, from_y).start()

    own = pltpu.make_async_copy(images, buf.at[pl.ds(2, 2), pl.ds(4, DEPTH)], local_sem)
    own.start()

    @pl.when(slab == 0)
    def _():
        buf[:, 0:4] = jnp.zeros((6, 4, CY, CX), jnp.float32)

    @pl.when(slab == slabs - 1)
    def _():
        buf[:, DEPTH + 4 : DEPTH + 8] = jnp.zeros((6, 4, CY, CX), jnp.float32)

    padded[:, 0:8, :] = jnp.zeros((FIELDS, 8, CX), jnp.float32)
    padded[:, 72:80, :] = jnp.zeros((FIELDS, 8, CX), jnp.float32)
    row = lax.broadcasted_iota(jnp.int32, (128, 128), 0)
    column = lax.broadcasted_iota(jnp.int32, (128, 128), 1)
    near = jnp.where(jnp.abs(row - column) <= 4, 1.0, 0.0).astype(jnp.bfloat16)
    for i in range(3):
        band[i * 128 : (i + 1) * 128, :] = near
    own.wait()
    for up in (0, 1):
        send_rims((0,), up, lambda copy: copy.start())

    def serve(k):
        x_copy(k, from_x).wait_recv()
        y_copy(k).start()

    def work(fields, at):
        plane_windows(fields, at, place, buf, padded, partial, operand, band, windows)

    def coefs_of(first, size):
        block_coefs(first, size, place, buf, windows, coef_ref)

    @pl.loop(0, DEPTH + LAG)
    def _(t):
        u = t - LAG

        @pl.when(t < DEPTH)
        def _():
            serve(t)
            work(SOON, plane_of(t) + 4)

        @pl.when(u >= 0)
        def _():
            y_copy(u).wait_recv()
            work(LATE, plane_of(u) + 4)

        for (which, up), step in SENT.items():
            @pl.when(u == step)
            def _():
                send_rims((which,), up, lambda copy: copy.start())

        for (which, up), slab_between in relays.items():
            @pl.when((u == SENT[which, up] + RELAY) & (slab == slab_between))
            def _():
                to_relay(which, up).wait_recv()
                from_relay(which, up).start()

        @pl.when(u == 8)
        def _():
            await_rims((0,), 0)
            await_rims((0,), 1)

        @pl.when((u >= 8) & (u < 16))
        def _():
            @pl.loop(0, 4)
            def _(q):
                plane_gradient((u - 8) * 4 + q, buf, gradient_ref)

        @pl.when(u == 16)
        def _():
            await_rims((1, 2), 1)

        @pl.when(u == 20)
        def _():
            await_rims((1, 2), 0)

        @pl.when((u >= 16) & (u < 24))
        def _():
            at = u - 16 + DEPTH * ((u - 16) // 4)
            work(SOON, at)
            work(LATE, at)

        for first, size, step in BLOCKS:
            @pl.when(u == step)
            def _():
                coefs_of(first, size)

    coefs_of(LAST, DEPTH - LAST)

    @pl.loop(0, DEPTH)
    def _(k):
        x_copy(k, from_y).wait_send()
        y_copy(k).wait_send()

    for up in (0, 1):
        send_rims((0, 1, 2), up, lambda copy: copy.wait_send())
    for (which, up), slab_between in relays.items():
        @pl.when(slab == slab_between)
        def _():
            from_relay(which, up).wait_send()


def plane_gradient(z, buf, gradient_ref):
    row = lax.broadcasted_iota(jnp.int32, (CY, CX), 0)
    column = lax.broadcasted_iota(jnp.int32, (CY, CX), 1)
    for p in range(2):
        half = buf[2 + p, z + 4] * 0.5
        gradient_ref[0, p, z] = 0.5 * (buf[2 + p, z + 5] - buf[2 + p, z + 3])
        up = jnp.where(row < CY - 1, pltpu.roll(half, CY - 1, 0), 0.0)
        down = jnp.where(row > 0, pltpu.roll(half, 1, 0), 0.0)
        gradient_ref[1, p, z] = up - down
        up = jnp.where(column < CX - 1, pltpu.roll(half, CX - 1, 1), 0.0)
        down = jnp.where(column > 0, pltpu.roll(half, 1, 1), 0.0)
        gradient_ref[2, p, z] = up - down


def force_kernel(coef, gradient, out_ref, out, sem):
    def copy(c):
        planes = pl.ds(c * STORE, STORE)
        return pltpu.make_async_copy(out.at[:, :, planes], out_ref.at[:, :, planes], sem.at[c])

    @pl.loop(0, DEPTH // STORE)
    def _(c):
        @pl.loop(0, STORE)
        def _(q):
            z = c * STORE + q
            for p in range(2):
                for k in range(3):
                    out[k, p, z] = coef[p, z] * gradient[k, p, z]

        copy(c).start()

    @pl.loop(0, DEPTH // STORE)
    def _(c):
        copy(c).wait()


def local(images):
    f32, vmem = jnp.float32, pl.BlockSpec(memory_space=pltpu.VMEM)
    dma = pltpu.SemaphoreType.DMA
    coefs, gradient = pl.pallas_call(
        coef_kernel,
        out_shape=(
            pltpu.VMEM((2, DEPTH, CY, CX), f32),
            pltpu.VMEM((3, 2, DEPTH, CY, CX), f32),
        ),
        in_specs=[pl.BlockSpec(memory_space=pltpu.HBM)],
        out_specs=(vmem, vmem),
        scratch_shapes=[
            pltpu.VMEM((6, DEPTH + 8, CY, CX), f32),
            pltpu.VMEM((FIELDS, 80, CX), f32),
            pltpu.VMEM((FIELDS, 72, CX), f32),
            pltpu.VMEM((FIELDS * CY, 384), jnp.bfloat16),
            pltpu.VMEM((384, CX), jnp.bfloat16),
            pltpu.VMEM((DEPTH + 8, FIELDS * CY, CX), f32),
            dma((DEPTH,)), dma((DEPTH,)), dma((DEPTH,)), dma((DEPTH,)),
            dma((3, 2)), dma((3, 2)), dma((3,)), dma, dma,
            pltpu.VMEM((2, 4, CY, CX), f32),
        ],
        compiler_params=pltpu.CompilerParams(
            collective_id=0, has_side_effects=True, vmem_limit_bytes=54 * 2**20
        ),
        name="coefs",
    )(images)
    return pl.pallas_call(
        force_kernel,
        out_shape=jax.ShapeDtypeStruct((3, 2, DEPTH, CY, CX), f32),
        in_specs=[vmem, vmem],
        out_specs=pl.BlockSpec(memory_space=pl.ANY),
        scratch_shapes=[pltpu.VMEM((3, 2, DEPTH, CY, CX), f32), dma((DEPTH // STORE,))],
        compiler_params=pltpu.CompilerParams(vmem_limit_bytes=16 * 2**20),
        name="forces",
    )(coefs, gradient)


def solution(mesh):
    in_specs = (P("phase", "slab", None, None),)
    out_specs = P(None, "phase", "slab", None, None)
    return jax.shard_map(local, mesh=mesh, in_specs=in_specs, out_specs=out_specs, check_vma=False)
```

```python
import jax
import jax.numpy as jnp
from jax import lax
from jax.experimental import pallas as pl
from jax.experimental.pallas import tpu as pltpu
from jax.sharding import PartitionSpec as P

EPSILON = 1e-05
MESH = pl.DeviceIdType.MESH
SOON = (0, 1, 2, 3, (0, 0), (1, 1), (2, 2), (3, 3), (0, 1), (0, 2), (1, 2), (1, 3))
LATE = (4, 5, (4, 4), (5, 5), (0, 5), (0, 4), (1, 5))
ORDER = SOON + LATE
PAIRS = tuple(f for f in ORDER if f not in range(6) and f[0] != f[1])
FIELDS = len(ORDER)
CY, CX = 64, 128
DEPTH = 32
SENT = {(1, 1): 0, (2, 1): 3, (1, 0): 4, (2, 0): 7}
RELAY = 6
BLOCKS = ((0, 7, 20), (7, 8, 24), (15, 4, 26), (19, 4, 30))
LAST = 23
STORES = ((0, 6), (6, 6), (12, 6), (18, 5))
LAG = 4


def plane_windows(fields, at, place, buf, padded, partial, operand, band, windows):
    base, count = ORDER.index(fields[0]), len(fields)
    images = {j: buf[place[j], at] for j in range(6) if any(j == f or f not in range(6) and j in f for f in fields)}
    for f, field in enumerate(fields, base):
        padded[f, 8:72, :] = images[field] if field in range(6) else images[field[0]] * images[field[1]]
    for f in range(base, base + count):
        partial[f] = padded[f, 3:75, :] + padded[f, 4:76, :] + padded[f, 5:77, :]
    for f in range(base, base + count):
        summed = partial[f, 1:65, :] + partial[f, 4:68, :] + partial[f, 7:71, :]
        high = summed.astype(jnp.bfloat16)
        rest = summed - high.astype(jnp.float32)
        middle = rest.astype(jnp.bfloat16)
        low = (rest - middle.astype(jnp.float32)).astype(jnp.bfloat16)
        rows = slice(f * CY, (f + 1) * CY)
        operand[rows, 0:128] = high
        operand[rows, 128:256] = middle
        operand[rows, 256:384] = low
    rows = slice(base * CY, (base + count) * CY)
    windows[at, rows] = jnp.dot(operand[rows, :], band[...], preferred_element_type=jnp.float32)


def block_coefs(first, size, place, buf, windows, coef_ref):
    @pl.loop(0, CY // 8)
    def _(r):
        sums = []
        for f in range(FIELDS):
            p = windows[pl.ds(first, size + 8), pl.ds(pl.multiple_of(f * CY + r * 8, 8), 8), :]
            common = p[size - 1]
            for i in range(size, 9):
                common = common + p[i]
            left, right = {}, {}
            for i in reversed(range(size - 1)):
                left[i] = p[i] + left[i + 1] if i + 1 in left else p[i]
            for i in range(1, size):
                right[i] = right[i - 1] + p[8 + i] if i - 1 in right else p[8 + i]
            sums.append([])
            for i in range(size):
                ends = [part[i] for part in (left, right) if i in part]
                sums[f].append(common + (ends[0] + ends[1] if len(ends) == 2 else ends[0]))
        tile = pl.ds(pl.multiple_of(r * 8, 8), 8)
        for i in range(size):
            total = {field: s[i] * (1.0 / 729.0) for field, s in zip(ORDER, sums)}
            spread = [total[j, j] - total[j] * total[j] for j in range(6)]
            offset = [buf[place[j], first + 4 + i, tile, :] - total[j] for j in range(6)]
            along, across = [0.0, 0.0], [0.0, 0.0]
            for a, b in PAIRS:
                covariance = total[a, b] - total[a] * total[b]
                weight = 2.0 * covariance / (spread[a] * spread[b] + EPSILON)
                scaled = weight * covariance
                for own, other in ((a, b), (b, a)):
                    if own < 2:
                        along[own] += weight * offset[other]
                        across[own] += scaled
            for own in (0, 1):
                coef_ref[place[own] - 2, first + i, tile, :] = (
                    along[own] - across[own] / (spread[own] + EPSILON) * offset[own]
                )


def places(side):
    from_x, from_y = 4 - 4 * side, 4 * side
    return (2 + side, 3 - side, from_x + side, from_x + 1 - side, from_y + side, from_y + 1 - side)


def coef_kernel(
    images, coef_ref, gradient_ref, buf, windows, padded, partial, operand, band,
    x_send, x_recv, y_send, y_recv, rim_send, rim_recv, relay_send, relay_recv, local_sem, relay,
):
    phase, slab = lax.axis_index("phase"), lax.axis_index("slab")
    slabs = lax.axis_size("slab")
    y, side = phase // 2, phase % 2
    partner = (y * 2 + 1 - side, slab)
    y_to = ((y + 1 + 2 * side) % 4 * 2 + side, slab)
    y_from = ((y + 3 + 2 * side) % 4 * 2 + side, slab)
    below = (phase, (slab + slabs - 1) % slabs)
    above = (phase, (slab + 1) % slabs)

    barrier = pltpu.get_barrier_semaphore()
    for peer in (partner, y_to, y_from, below, above):
        pl.semaphore_signal(barrier, inc=1, device_id=peer, device_id_type=MESH)

    middle = slabs // 2
    relays = {(1, 1): middle + 2, (2, 1): slabs - 4, (1, 0): middle - 3, (2, 0): 3}
    ends = (slab == middle - 1) | (slab == middle)
    passes = (slab == middle + 2) | (slab == slabs - 4) | (slab == middle - 3) | (slab == 3)

    @pl.when(ends)
    def _():
        for peer in relays.values():
            pl.semaphore_signal(barrier, inc=1, device_id=(phase, peer), device_id_type=MESH)
        pl.semaphore_wait(barrier, 9)

    @pl.when(passes)
    def _():
        for peer in (middle - 1, middle):
            pl.semaphore_signal(barrier, inc=1, device_id=(phase, peer), device_id_type=MESH)
        pl.semaphore_wait(barrier, 7)

    @pl.when(jnp.logical_not(ends | passes))
    def _():
        pl.semaphore_wait(barrier, 5)

    from_x, from_y = 4 - 4 * side, 4 * side
    place = places(side)

    def plane_of(k):
        return (k + DEPTH - 4) % DEPTH

    def x_copy(k, slot):
        z = plane_of(k)
        return pltpu.make_async_remote_copy(
            images.at[:, pl.ds(z, 1)], buf.at[pl.ds(slot, 2), pl.ds(4 + z, 1)],
            x_send.at[k], x_recv.at[k], device_id=partner, device_id_type=MESH,
        )

    def y_copy(k):
        z = plane_of(k)
        return pltpu.make_async_remote_copy(
            buf.at[pl.ds(from_x, 2), pl.ds(4 + z, 1)], buf.at[pl.ds(from_y, 2), pl.ds(4 + z, 1)],
            y_send.at[k], y_recv.at[k], device_id=y_to, device_id_type=MESH,
        )

    def rim_copy(which, up):
        slot = (2, from_x, from_y)[which]
        source = pl.ds(DEPTH, 4) if up else pl.ds(4, 4)
        target = pl.ds(0, 4) if up else pl.ds(DEPTH + 4, 4)
        return pltpu.make_async_remote_copy(
            buf.at[pl.ds(slot, 2), source], buf.at[pl.ds(slot, 2), target],
            rim_send.at[which, up], rim_recv.at[which, up],
            device_id=above if up else below, device_id_type=MESH,
        )

    def to_relay(which, up):
        slot = (2, from_x, from_y)[which]
        return pltpu.make_async_remote_copy(
            buf.at[pl.ds(slot, 2), pl.ds(DEPTH, 4) if up else pl.ds(4, 4)], relay,
            relay_send.at[which], relay_recv, device_id=(phase, relays[which, up]), device_id_type=MESH,
        )

    def from_relay(which, up):
        slot = (2, from_x, from_y)[which]
        return pltpu.make_async_remote_copy(
            relay, buf.at[pl.ds(slot, 2), pl.ds(0, 4) if up else pl.ds(DEPTH + 4, 4)],
            relay_send.at[0], rim_recv.at[which, up],
            device_id=(phase, middle if up else middle - 1), device_id_type=MESH,
        )

    def send_rims(whiches, up, act):
        edge, end = (slabs - 1, middle - 1) if up else (0, middle)

        @pl.when((slab != edge) & (slab != end))
        def _():
            for which in whiches:
                act(rim_copy(which, up))

        @pl.when(slab == end)
        def _():
            for which in whiches:
                act(to_relay(which, up) if which else rim_copy(which, up))

    def await_rims(whiches, up):
        @pl.when(slab != (0 if up else slabs - 1))
        def _():
            for which in whiches:
                rim_copy(which, up).wait_recv()

    @pl.loop(0, DEPTH)
    def _(k):
        x_copy(k, from_y).start()

    own = pltpu.make_async_copy(images, buf.at[pl.ds(2, 2), pl.ds(4, DEPTH)], local_sem)
    own.start()

    @pl.when(slab == 0)
    def _():
        buf[:, 0:4] = jnp.zeros((6, 4, CY, CX), jnp.float32)

    @pl.when(slab == slabs - 1)
    def _():
        buf[:, DEPTH + 4 : DEPTH + 8] = jnp.zeros((6, 4, CY, CX), jnp.float32)

    padded[:, 0:8, :] = jnp.zeros((FIELDS, 8, CX), jnp.float32)
    padded[:, 72:80, :] = jnp.zeros((FIELDS, 8, CX), jnp.float32)
    row = lax.broadcasted_iota(jnp.int32, (128, 128), 0)
    column = lax.broadcasted_iota(jnp.int32, (128, 128), 1)
    near = jnp.where(jnp.abs(row - column) <= 4, 1.0, 0.0).astype(jnp.bfloat16)
    for i in range(3):
        band[i * 128 : (i + 1) * 128, :] = near
    own.wait()
    for up in (0, 1):
        send_rims((0,), up, lambda copy: copy.start())

    def serve(k):
        x_copy(k, from_x).wait_recv()
        y_copy(k).start()

    def work(fields, at):
        plane_windows(fields, at, place, buf, padded, partial, operand, band, windows)

    def coefs_of(first, size):
        block_coefs(first, size, place, buf, windows, coef_ref)

    @pl.loop(0, DEPTH + LAG)
    def _(t):
        u = t - LAG

        @pl.when(t < DEPTH)
        def _():
            serve(t)
            work(SOON, plane_of(t) + 4)

        @pl.when(u >= 0)
        def _():
            y_copy(u).wait_recv()
            work(LATE, plane_of(u) + 4)

        for (which, up), step in SENT.items():
            @pl.when(u == step)
            def _():
                send_rims((which,), up, lambda copy: copy.start())

        for (which, up), slab_between in relays.items():
            @pl.when((u == SENT[which, up] + RELAY) & (slab == slab_between))
            def _():
                to_relay(which, up).wait_recv()
                from_relay(which, up).start()

        @pl.when(u == 8)
        def _():
            await_rims((0,), 0)
            await_rims((0,), 1)

        @pl.when((u >= 8) & (u < 16))
        def _():
            @pl.loop(0, 4)
            def _(q):
                plane_gradient((u - 8) * 4 + q, buf, gradient_ref)

        @pl.when(u == 16)
        def _():
            await_rims((1, 2), 1)

        @pl.when(u == 20)
        def _():
            await_rims((1, 2), 0)

        @pl.when((u >= 16) & (u < 24))
        def _():
            at = u - 16 + DEPTH * ((u - 16) // 4)
            work(SOON, at)
            work(LATE, at)

        for first, size, step in BLOCKS:
            @pl.when(u == step)
            def _():
                coefs_of(first, size)

    @pl.loop(0, DEPTH)
    def _(k):
        x_copy(k, from_y).wait_send()
        y_copy(k).wait_send()

    for up in (0, 1):
        send_rims((0, 1, 2), up, lambda copy: copy.wait_send())
    for (which, up), slab_between in relays.items():
        @pl.when(slab == slab_between)
        def _():
            from_relay(which, up).wait_send()


def plane_gradient(z, buf, gradient_ref):
    row = lax.broadcasted_iota(jnp.int32, (CY, CX), 0)
    column = lax.broadcasted_iota(jnp.int32, (CY, CX), 1)
    for p in range(2):
        half = buf[2 + p, z + 4] * 0.5
        gradient_ref[0, p, z] = 0.5 * (buf[2 + p, z + 5] - buf[2 + p, z + 3])
        up = jnp.where(row < CY - 1, pltpu.roll(half, CY - 1, 0), 0.0)
        down = jnp.where(row > 0, pltpu.roll(half, 1, 0), 0.0)
        gradient_ref[1, p, z] = up - down
        up = jnp.where(column < CX - 1, pltpu.roll(half, CX - 1, 1), 0.0)
        down = jnp.where(column > 0, pltpu.roll(half, 1, 1), 0.0)
        gradient_ref[2, p, z] = up - down


def force_kernel(coef, gradient, buf, windows, out_ref, late, out, sem):
    def store(i, first, size, coefs):
        @pl.loop(first, first + size)
        def _(z):
            for p in range(2):
                for k in range(3):
                    out[k, p, z] = coefs[p, z] * gradient[k, p, z]

        planes = pl.ds(first, size)
        copy = pltpu.make_async_copy(out.at[:, :, planes], out_ref.at[:, :, planes], sem.at[i])
        copy.start()
        return copy

    copies = [store(i, first, size, coef) for i, (first, size) in enumerate(STORES)]
    block_coefs(LAST, DEPTH - LAST, places(lax.axis_index("phase") % 2), buf, windows, late)
    copies.append(store(len(STORES), LAST, DEPTH - LAST, late))
    for copy in copies:
        copy.wait()


def local(images):
    f32, vmem = jnp.float32, pl.BlockSpec(memory_space=pltpu.VMEM)
    dma = pltpu.SemaphoreType.DMA
    results = pl.pallas_call(
        coef_kernel,
        out_shape=(
            pltpu.VMEM((2, DEPTH, CY, CX), f32),
            pltpu.VMEM((3, 2, DEPTH, CY, CX), f32),
            pltpu.VMEM((6, DEPTH + 8, CY, CX), f32),
            pltpu.VMEM((DEPTH + 8, FIELDS * CY, CX), f32),
        ),
        in_specs=[pl.BlockSpec(memory_space=pltpu.HBM)],
        out_specs=(vmem,) * 4,
        scratch_shapes=[
            pltpu.VMEM((FIELDS, 80, CX), f32),
            pltpu.VMEM((FIELDS, 72, CX), f32),
            pltpu.VMEM((FIELDS * CY, 384), jnp.bfloat16),
            pltpu.VMEM((384, CX), jnp.bfloat16),
            dma((DEPTH,)), dma((DEPTH,)), dma((DEPTH,)), dma((DEPTH,)),
            dma((3, 2)), dma((3, 2)), dma((3,)), dma, dma,
            pltpu.VMEM((2, 4, CY, CX), f32),
        ],
        compiler_params=pltpu.CompilerParams(
            collective_id=0, has_side_effects=True, vmem_limit_bytes=20 * 2**20
        ),
        name="coefs",
    )(images)
    return pl.pallas_call(
        force_kernel,
        out_shape=jax.ShapeDtypeStruct((3, 2, DEPTH, CY, CX), f32),
        in_specs=[vmem] * 4,
        out_specs=pl.BlockSpec(memory_space=pl.ANY),
        scratch_shapes=[pltpu.VMEM((2, DEPTH, CY, CX), f32), pltpu.VMEM((3, 2, DEPTH, CY, CX), f32), dma((len(STORES) + 1,))],
        compiler_params=pltpu.CompilerParams(vmem_limit_bytes=10 * 2**20),
        name="forces",
    )(*results)


def solution(mesh):
    in_specs = (P("phase", "slab", None, None),)
    out_specs = P(None, "phase", "slab", None, None)
    return jax.shard_map(local, mesh=mesh, in_specs=in_specs, out_specs=out_specs, check_vma=False)
```

```python
import jax
import jax.numpy as jnp
from jax import lax
from jax.experimental import pallas as pl
from jax.experimental.pallas import tpu as pltpu
from jax.sharding import PartitionSpec as P

EPSILON = 1e-05
MESH = pl.DeviceIdType.MESH
SOON = (0, 1, 2, 3, (0, 0), (1, 1), (2, 2), (3, 3), (0, 1), (0, 2), (1, 2), (1, 3))
LATE = (4, 5, (4, 4), (5, 5), (0, 5), (0, 4), (1, 5))
ORDER = SOON + LATE
PAIRS = tuple(f for f in ORDER if f not in range(6) and f[0] != f[1])
FIELDS = len(ORDER)
CY, CX = 64, 128
DEPTH = 32
SENT = {(1, 1): 0, (2, 1): 3, (1, 0): 4, (2, 0): 7}
RELAY = 5
BLOCKS = ((0, 7, 17), (7, 8, 22), (15, 8, 30))
LAST = 23
STORES = ((0, 6), (6, 6), (12, 6), (18, 5))
LAG = 4


def plane_windows(fields, at, place, buf, padded, partial, operand, band, windows):
    base, count = ORDER.index(fields[0]), len(fields)
    images = {j: buf[place[j], at] for j in range(6) if any(j == f or f not in range(6) and j in f for f in fields)}
    for f, field in enumerate(fields, base):
        padded[f, 8:72, :] = images[field] if field in range(6) else images[field[0]] * images[field[1]]
    for f in range(base, base + count):
        partial[f] = padded[f, 3:75, :] + padded[f, 4:76, :] + padded[f, 5:77, :]
    for f in range(base, base + count):
        summed = partial[f, 1:65, :] + partial[f, 4:68, :] + partial[f, 7:71, :]
        high = summed.astype(jnp.bfloat16)
        rest = summed - high.astype(jnp.float32)
        middle = rest.astype(jnp.bfloat16)
        low = (rest - middle.astype(jnp.float32)).astype(jnp.bfloat16)
        rows = slice(f * CY, (f + 1) * CY)
        operand[rows, 0:128] = high
        operand[rows, 128:256] = middle
        operand[rows, 256:384] = low
    rows = slice(base * CY, (base + count) * CY)
    windows[at, rows] = jnp.dot(operand[rows, :], band[...], preferred_element_type=jnp.float32)


def block_coefs(first, size, place, buf, windows, coef_ref):
    @pl.loop(0, CY // 8)
    def _(r):
        sums = []
        for f in range(FIELDS):
            p = windows[pl.ds(first, size + 8), pl.ds(pl.multiple_of(f * CY + r * 8, 8), 8), :]
            common = p[size - 1]
            for i in range(size, 9):
                common = common + p[i]
            left, right = {}, {}
            for i in reversed(range(size - 1)):
                left[i] = p[i] + left[i + 1] if i + 1 in left else p[i]
            for i in range(1, size):
                right[i] = right[i - 1] + p[8 + i] if i - 1 in right else p[8 + i]
            sums.append([])
            for i in range(size):
                ends = [part[i] for part in (left, right) if i in part]
                sums[f].append(common + (ends[0] + ends[1] if len(ends) == 2 else ends[0]))
        tile = pl.ds(pl.multiple_of(r * 8, 8), 8)
        for i in range(size):
            total = {field: s[i] * (1.0 / 729.0) for field, s in zip(ORDER, sums)}
            spread = [total[j, j] - total[j] * total[j] for j in range(6)]
            offset = [buf[place[j], first + 4 + i, tile, :] - total[j] for j in range(6)]
            along, across = [0.0, 0.0], [0.0, 0.0]
            for a, b in PAIRS:
                covariance = total[a, b] - total[a] * total[b]
                weight = 2.0 * covariance / (spread[a] * spread[b] + EPSILON)
                scaled = weight * covariance
                for own, other in ((a, b), (b, a)):
                    if own < 2:
                        along[own] += weight * offset[other]
                        across[own] += scaled
            for own in (0, 1):
                coef_ref[place[own] - 2, first + i, tile, :] = (
                    along[own] - across[own] / (spread[own] + EPSILON) * offset[own]
                )


def places(side):
    from_x, from_y = 4 - 4 * side, 4 * side
    return (2 + side, 3 - side, from_x + side, from_x + 1 - side, from_y + side, from_y + 1 - side)


def coef_kernel(
    images, coef_ref, gradient_ref, buf, windows, padded, partial, operand, band,
    x_send, x_recv, y_send, y_recv, rim_send, rim_recv, relay_send, relay_recv, local_sem, relay,
):
    phase, slab = lax.axis_index("phase"), lax.axis_index("slab")
    slabs = lax.axis_size("slab")
    y, side = phase // 2, phase % 2
    partner = (y * 2 + 1 - side, slab)
    y_to = ((y + 1 + 2 * side) % 4 * 2 + side, slab)
    y_from = ((y + 3 + 2 * side) % 4 * 2 + side, slab)
    below = (phase, (slab + slabs - 1) % slabs)
    above = (phase, (slab + 1) % slabs)

    barrier = pltpu.get_barrier_semaphore()
    for peer in (partner, y_to, y_from, below, above):
        pl.semaphore_signal(barrier, inc=1, device_id=peer, device_id_type=MESH)

    middle = slabs // 2
    relays = {(1, 1): middle + 2, (2, 1): slabs - 4, (1, 0): middle - 3, (2, 0): 3}
    ends = (slab == middle - 1) | (slab == middle)
    passes = (slab == middle + 2) | (slab == slabs - 4) | (slab == middle - 3) | (slab == 3)

    @pl.when(ends)
    def _():
        for peer in relays.values():
            pl.semaphore_signal(barrier, inc=1, device_id=(phase, peer), device_id_type=MESH)
        pl.semaphore_wait(barrier, 9)

    @pl.when(passes)
    def _():
        for peer in (middle - 1, middle):
            pl.semaphore_signal(barrier, inc=1, device_id=(phase, peer), device_id_type=MESH)
        pl.semaphore_wait(barrier, 7)

    @pl.when(jnp.logical_not(ends | passes))
    def _():
        pl.semaphore_wait(barrier, 5)

    from_x, from_y = 4 - 4 * side, 4 * side
    place = places(side)

    def plane_of(k):
        return (k + DEPTH - 4) % DEPTH

    def x_copy(k, slot):
        z = plane_of(k)
        return pltpu.make_async_remote_copy(
            images.at[:, pl.ds(z, 1)], buf.at[pl.ds(slot, 2), pl.ds(4 + z, 1)],
            x_send.at[k], x_recv.at[k], device_id=partner, device_id_type=MESH,
        )

    def y_copy(k):
        z = plane_of(k)
        return pltpu.make_async_remote_copy(
            buf.at[pl.ds(from_x, 2), pl.ds(4 + z, 1)], buf.at[pl.ds(from_y, 2), pl.ds(4 + z, 1)],
            y_send.at[k], y_recv.at[k], device_id=y_to, device_id_type=MESH,
        )

    def rim_copy(which, up):
        slot = (2, from_x, from_y)[which]
        source = pl.ds(DEPTH, 4) if up else pl.ds(4, 4)
        target = pl.ds(0, 4) if up else pl.ds(DEPTH + 4, 4)
        return pltpu.make_async_remote_copy(
            buf.at[pl.ds(slot, 2), source], buf.at[pl.ds(slot, 2), target],
            rim_send.at[which, up], rim_recv.at[which, up],
            device_id=above if up else below, device_id_type=MESH,
        )

    def to_relay(which, up):
        slot = (2, from_x, from_y)[which]
        return pltpu.make_async_remote_copy(
            buf.at[pl.ds(slot, 2), pl.ds(DEPTH, 4) if up else pl.ds(4, 4)], relay,
            relay_send.at[which], relay_recv, device_id=(phase, relays[which, up]), device_id_type=MESH,
        )

    def from_relay(which, up):
        slot = (2, from_x, from_y)[which]
        return pltpu.make_async_remote_copy(
            relay, buf.at[pl.ds(slot, 2), pl.ds(0, 4) if up else pl.ds(DEPTH + 4, 4)],
            relay_send.at[0], rim_recv.at[which, up],
            device_id=(phase, middle if up else middle - 1), device_id_type=MESH,
        )

    def send_rims(whiches, up, act):
        edge, end = (slabs - 1, middle - 1) if up else (0, middle)

        @pl.when((slab != edge) & (slab != end))
        def _():
            for which in whiches:
                act(rim_copy(which, up))

        @pl.when(slab == end)
        def _():
            for which in whiches:
                act(to_relay(which, up) if which else rim_copy(which, up))

    def await_rims(whiches, up):
        @pl.when(slab != (0 if up else slabs - 1))
        def _():
            for which in whiches:
                rim_copy(which, up).wait_recv()

    @pl.loop(0, DEPTH)
    def _(k):
        x_copy(k, from_y).start()

    own = pltpu.make_async_copy(images, buf.at[pl.ds(2, 2), pl.ds(4, DEPTH)], local_sem)
    own.start()

    @pl.when(slab == 0)
    def _():
        buf[:, 0:4] = jnp.zeros((6, 4, CY, CX), jnp.float32)

    @pl.when(slab == slabs - 1)
    def _():
        buf[:, DEPTH + 4 : DEPTH + 8] = jnp.zeros((6, 4, CY, CX), jnp.float32)

    padded[:, 0:8, :] = jnp.zeros((FIELDS, 8, CX), jnp.float32)
    padded[:, 72:80, :] = jnp.zeros((FIELDS, 8, CX), jnp.float32)
    row = lax.broadcasted_iota(jnp.int32, (128, 128), 0)
    column = lax.broadcasted_iota(jnp.int32, (128, 128), 1)
    near = jnp.where(jnp.abs(row - column) <= 4, 1.0, 0.0).astype(jnp.bfloat16)
    for i in range(3):
        band[i * 128 : (i + 1) * 128, :] = near
    own.wait()
    for up in (0, 1):
        send_rims((0,), up, lambda copy: copy.start())

    def serve(k):
        x_copy(k, from_x).wait_recv()
        y_copy(k).start()

    def work(fields, at):
        plane_windows(fields, at, place, buf, padded, partial, operand, band, windows)

    def coefs_of(first, size):
        block_coefs(first, size, place, buf, windows, coef_ref)

    @pl.loop(0, DEPTH + LAG)
    def _(t):
        u = t - LAG

        @pl.when(t < DEPTH)
        def _():
            serve(t)
            work(SOON, plane_of(t) + 4)

        @pl.when(u >= 0)
        def _():
            y_copy(u).wait_recv()
            work(LATE, plane_of(u) + 4)

        for (which, up), step in SENT.items():
            @pl.when(u == step)
            def _():
                send_rims((which,), up, lambda copy: copy.start())

        for (which, up), slab_between in relays.items():
            @pl.when((u == SENT[which, up] + RELAY) & (slab == slab_between))
            def _():
                to_relay(which, up).wait_recv()
                from_relay(which, up).start()

        @pl.when(u == 8)
        def _():
            await_rims((0,), 0)
            await_rims((0,), 1)

        @pl.when((u >= 8) & (u < 16))
        def _():
            @pl.loop(0, 4)
            def _(q):
                plane_gradient((u - 8) * 4 + q, buf, gradient_ref)

        @pl.when(u == 13)
        def _():
            await_rims((1, 2), 1)

        @pl.when(u == 17)
        def _():
            await_rims((1, 2), 0)

        @pl.when((u >= 13) & (u < 21))
        def _():
            at = u - 13 + DEPTH * ((u - 13) // 4)
            work(SOON, at)
            work(LATE, at)

        for first, size, step in BLOCKS:
            @pl.when(u == step)
            def _():
                coefs_of(first, size)

    @pl.loop(0, DEPTH)
    def _(k):
        x_copy(k, from_y).wait_send()
        y_copy(k).wait_send()

    for up in (0, 1):
        send_rims((0, 1, 2), up, lambda copy: copy.wait_send())
    for (which, up), slab_between in relays.items():
        @pl.when(slab == slab_between)
        def _():
            from_relay(which, up).wait_send()


def plane_gradient(z, buf, gradient_ref):
    row = lax.broadcasted_iota(jnp.int32, (CY, CX), 0)
    column = lax.broadcasted_iota(jnp.int32, (CY, CX), 1)
    for p in range(2):
        half = buf[2 + p, z + 4] * 0.5
        gradient_ref[0, p, z] = 0.5 * (buf[2 + p, z + 5] - buf[2 + p, z + 3])
        up = jnp.where(row < CY - 1, pltpu.roll(half, CY - 1, 0), 0.0)
        down = jnp.where(row > 0, pltpu.roll(half, 1, 0), 0.0)
        gradient_ref[1, p, z] = up - down
        up = jnp.where(column < CX - 1, pltpu.roll(half, CX - 1, 1), 0.0)
        down = jnp.where(column > 0, pltpu.roll(half, 1, 1), 0.0)
        gradient_ref[2, p, z] = up - down


def force_kernel(coef, gradient, buf, windows, out_ref, late, out, sem):
    def store(i, first, size, coefs):
        @pl.loop(first, first + size)
        def _(z):
            for p in range(2):
                for k in range(3):
                    out[k, p, z] = coefs[p, z] * gradient[k, p, z]

        planes = pl.ds(first, size)
        copy = pltpu.make_async_copy(out.at[:, :, planes], out_ref.at[:, :, planes], sem.at[i])
        copy.start()
        return copy

    copies = [store(i, first, size, coef) for i, (first, size) in enumerate(STORES)]
    block_coefs(LAST, DEPTH - LAST, places(lax.axis_index("phase") % 2), buf, windows, late)
    copies.append(store(len(STORES), LAST, DEPTH - LAST, late))
    for copy in copies:
        copy.wait()


def local(images):
    f32, vmem = jnp.float32, pl.BlockSpec(memory_space=pltpu.VMEM)
    dma = pltpu.SemaphoreType.DMA
    results = pl.pallas_call(
        coef_kernel,
        out_shape=(
            pltpu.VMEM((2, DEPTH, CY, CX), f32),
            pltpu.VMEM((3, 2, DEPTH, CY, CX), f32),
            pltpu.VMEM((6, DEPTH + 8, CY, CX), f32),
            pltpu.VMEM((DEPTH + 8, FIELDS * CY, CX), f32),
        ),
        in_specs=[pl.BlockSpec(memory_space=pltpu.HBM)],
        out_specs=(vmem,) * 4,
        scratch_shapes=[
            pltpu.VMEM((FIELDS, 80, CX), f32),
            pltpu.VMEM((FIELDS, 72, CX), f32),
            pltpu.VMEM((FIELDS * CY, 384), jnp.bfloat16),
            pltpu.VMEM((384, CX), jnp.bfloat16),
            dma((DEPTH,)), dma((DEPTH,)), dma((DEPTH,)), dma((DEPTH,)),
            dma((3, 2)), dma((3, 2)), dma((3,)), dma, dma,
            pltpu.VMEM((2, 4, CY, CX), f32),
        ],
        compiler_params=pltpu.CompilerParams(
            collective_id=0, has_side_effects=True, vmem_limit_bytes=20 * 2**20
        ),
        name="coefs",
    )(images)
    return pl.pallas_call(
        force_kernel,
        out_shape=jax.ShapeDtypeStruct((3, 2, DEPTH, CY, CX), f32),
        in_specs=[vmem] * 4,
        out_specs=pl.BlockSpec(memory_space=pl.ANY),
        scratch_shapes=[pltpu.VMEM((2, DEPTH, CY, CX), f32), pltpu.VMEM((3, 2, DEPTH, CY, CX), f32), dma((len(STORES) + 1,))],
        compiler_params=pltpu.CompilerParams(vmem_limit_bytes=10 * 2**20),
        name="forces",
    )(*results)


def solution(mesh):
    in_specs = (P("phase", "slab", None, None),)
    out_specs = P(None, "phase", "slab", None, None)
    return jax.shard_map(local, mesh=mesh, in_specs=in_specs, out_specs=out_specs, check_vma=False)
```
